32 devices in a mesh: asm: 8 (over y, x, core), amp: 4 (over z).
Axes of the slice: x: 2, y: 2, z: 4, core: 2. Of those that a mesh axis runs over, the one named last changes fastest.
Arguments:
- factors: bfloat16 [8, 3072, 1024], P('asm'), may hold values from -0.109375 to 0.109375
- amplitudes: bfloat16 [8, 1024, 1024], P(None, 'amp'), may hold values from -3 to 3
- eps_vir: float32 [1024], replicated, may hold values from 0.3 to 3
- pair_energy: float32 [8], P('amp'), may hold values from -2.5 to -0.5
- win_ids: int32 [8], replicated, may hold values from 0 to 1023, as said below
- block_count: int32 [8], P('asm'), may hold values from 1 to 2, as said below
Outputs:
- update: float32 [8, 8, 2], P('amp', 'asm')
The draws below stay inside these ranges and needn't reach their ends.
Inputs may be any that keep to these rules, and one draw needn't show every extreme that they name: `win_ids`: distinct values; both 0 and 1023 occur in every draw. `block_count`: slots 0 and 7 have 2, and some other slot has 1, in every draw.
All inputs are finite; a program needn't handle non-finite values.
Results may differ from the reference program's by a relative error of at most 0.003.
Values may be sent and summed in bfloat16 or wider, within the bound.
No kernel may reach another device: no remote copies, remote signals or barrier semaphores. Data moves between devices by JAX's collectives and lax.ppermute only.
A program may use at most 64 MiB of HBM per device.

```python
import jax
import jax.numpy as jnp
from jax import lax

V = 1024
NAUX = 3072
MB = 2
OPAIR = 8
NWIN = 8


def swap_into(order, value, position):
    inverse = jnp.argsort(order)
    location = inverse[value]
    held = order[position]
    return order.at[location].set(held).at[position].set(value)


def draw_win_ids(key, part):
    perm_key, first_key, second_key = jax.random.split(key, 3)
    order = jax.random.permutation(perm_key, V).astype(jnp.int32)
    high_slot = jax.random.randint(first_key, (), 0, NWIN)
    low_slot = (high_slot + jax.random.randint(second_key, (), 1, NWIN)) % NWIN
    order = swap_into(order, V - 1, high_slot)
    order = swap_into(order, 0, low_slot)
    return order[:NWIN].astype(jnp.int32)


def draw_block_count(key, part):
    first_key, second_key = jax.random.split(key, 2)
    counts = jax.random.randint(first_key, (NWIN,), 1, MB + 1)
    single = jax.random.randint(second_key, (), 1, NWIN - 1)
    counts = counts.at[0].set(MB).at[NWIN - 1].set(MB).at[single].set(1)
    return counts.astype(jnp.int32)


def levels(stream_key, shape, cuts, low, top_value):
    def one(axis_at, shards_of):
        heights = jax.random.uniform(jax.random.fold_in(jax.random.fold_in(stream_key, 6), axis_at), (shards_of,), jnp.float32, low / len(cuts), top_value / len(cuts))
        return jnp.repeat(jnp.exp(heights), shape[axis_at] // shards_of).reshape((-1,) + (1,) * (len(shape) - axis_at - 1))

    factor_of = one(*cuts[0])
    for cut in cuts[1:]:
        factor_of = factor_of * one(*cut)
    return factor_of


def gaussian(stream_key, shape, scale, reach, shards=(), kind=jnp.bfloat16):
    gain = levels(stream_key, shape, shards, -0.22, 0.18) if shards else 1.0
    values = jax.random.normal(stream_key, shape, jnp.float32) * scale * gain
    return jnp.minimum(jnp.maximum(values, -reach), reach).astype(kind)


def setup_inputs(seed: int = 0) -> dict:
    keys = jax.random.split(jax.random.key(seed), 7)
    return {
        "factors": gaussian(keys[0], (NWIN, NAUX, V), NAUX ** -0.5, 0.109375, ((0, 8),)),
        "amplitudes": gaussian(keys[1], (OPAIR, V, V), 0.2, 3.0, ((1, 4),)),
        "eps_vir": jnp.clip(jax.random.uniform(keys[2], (V,), jnp.float32, 0.3, 3.0), 0.3, 3.0),
        "pair_energy": jnp.clip(-2.5 + 2.0 * jax.random.uniform(keys[3], (OPAIR,), jnp.float32) ** levels(keys[3], (OPAIR,), ((0, 4),), -0.2, 0.2), -2.5, -0.5),
        "win_ids": draw_win_ids(jax.random.fold_in(keys[6], 71), 0),
        "block_count": draw_block_count(jax.random.fold_in(keys[6], 71), 0),
    }


def reference(factors, amplitudes, eps_vir, pair_energy, win_ids, block_count):
    windows = factors.shape[0]
    flat_amp = amplitudes.reshape(amplitudes.shape[0], V * V)
    eps_window = eps_vir[win_ids]

    def one_slot(slot):
        own_panel = factors[slot]
        columns = []
        for batch_index in range(MB):
            other = ((slot - batch_index - 1) % windows).astype(jnp.int32)
            product = lax.dot_general(factors[other], own_panel, (((0,), (0,)), ((), ())), preferred_element_type=jnp.float32)
            integral_tile = product.astype(jnp.bfloat16).reshape(V * V)
            resid = jnp.dot(flat_amp, integral_tile, preferred_element_type=jnp.float32)
            denom = pair_energy - eps_window[other] - eps_window[slot]
            columns.append(jnp.where(batch_index < block_count[slot], resid / denom, jnp.float32(0.0)))
        return jnp.stack(columns, axis=1)

    stacked = lax.map(one_slot, jnp.arange(windows, dtype=jnp.int32))
    return jnp.transpose(stacked, (1, 0, 2))
```

```python
import jax
import jax.numpy as jnp
from jax import lax
from jax.sharding import PartitionSpec as P

MB = 2


def from_behind(array, axis, by):
    peers = lax.axis_size(axis)
    return lax.ppermute(array, axis, [(i, (i + by) % peers) for i in range(peers)])


def lookup(table, position):
    places = jnp.arange(table.shape[0], dtype=jnp.int32)
    return jnp.sum(jnp.where(places == position, table, jnp.zeros_like(table)))


def cuts(total, parts):
    whole = sum(parts)
    edges, at = [], 0
    for part in parts:
        size = total * part // whole
        edges.append((at, size))
        at += size
    return edges


def contract(piece, panel):
    return lax.dot_general(
        piece, panel, (((0,), (0,)), ((), ())), preferred_element_type=jnp.float32
    )


def residual_of(amplitudes, tile):
    return jnp.sum(amplitudes.astype(jnp.float32) * tile[None], axis=(1, 2))


def share_sum(partial, axis):
    peers = lax.axis_size(axis)
    rank = lax.axis_index(axis)
    rows = partial.shape[0] // peers
    total = lax.dynamic_slice_in_dim(partial, rank * rows, rows, 0)
    for by in range(1, peers):
        to = (rank + by) % peers
        block = lax.dynamic_slice_in_dim(partial, to * rows, rows, 0)
        total = total + from_behind(block, axis, by)
    return total


def local(factors, amplitudes, eps_vir, pair_energy, win_ids, block_count):
    windows = win_ids.shape[0]
    quarter = amplitudes.shape[1]
    own_panel = factors[0]
    aux = own_panel.shape[0]
    rank_amp = lax.axis_index("amp")
    rank_asm = lax.axis_index("asm")

    first_cuts = cuts(aux, (1, 1, 1, 1))
    held = []
    for at, size in first_cuts:
        strip = lax.dynamic_slice(own_panel, (at, rank_amp * quarter), (size, quarter))
        held.append(from_behind(strip, "asm", 1))
    further = [from_behind(piece, "asm", 1) for piece in held]
    residuals = []
    for pieces in (held, further):
        tile = sum(
            contract(piece, own_panel[at : at + size])
            for piece, (at, size) in zip(pieces, first_cuts)
        )
        tile = tile.astype(jnp.bfloat16).astype(jnp.float32)
        residuals.append(residual_of(amplitudes, tile))
    partial = jnp.stack(residuals, axis=1)
    residual = share_sum(partial, "amp")

    own_energy = lookup(eps_vir, lookup(win_ids, rank_asm))
    other_energy = []
    for batch_index in range(MB):
        other_slot = (rank_asm - batch_index - 1) % windows
        other_energy.append(lookup(eps_vir, lookup(win_ids, other_slot)))
    other_energy = jnp.stack(other_energy)
    denom = pair_energy[:, None] - other_energy[None, :] - own_energy
    live = jnp.arange(MB, dtype=jnp.int32) < block_count[0]
    update = jnp.where(live[None, :], residual / denom, jnp.float32(0.0))
    return update[:, None, :]


def solution(mesh):
    in_specs = (P("asm", None, None), P(None, "amp", None), P(), P("amp"), P(), P("asm"))
    out_specs = P("amp", "asm", None)
    return jax.shard_map(local, mesh=mesh, in_specs=in_specs, out_specs=out_specs, check_vma=False)
```
